256 devices in a mesh: group: 16 (over y, x), member: 16 (over z, core).
Axes of the slice: x: 4, y: 4, z: 8, core: 2. Of those that a mesh axis runs over, the one named last changes fastest.
Arguments:
- level_set: bfloat16 [2048, 128, 2048], P(('group', 'member')), may hold values from -6 to 6
- ray_length: int32 [128, 2048], replicated, may hold values from 512 to 2048
- member_flip: int32 [16], P('group'), may hold values from 0 to 15
- group_flip: int32 [1], replicated, may hold values from 0 to 255
Outputs:
- final_image: float32 [5, 262144], P(None, ('group', 'member'))
The draws below stay inside these ranges and needn't reach their ends.
Inputs may be any that keep to these rules, and one draw needn't show every extreme that they name: `ray_length`: each entry is a ray's length in depth samples. `member_flip`: bit patterns of the viewing direction along the splits inside a block. `group_flip`: bit pattern of the viewing direction along all splits.
All inputs are finite; a program needn't handle non-finite values.
Results may differ from the reference program's by a relative error of at most 0.0003.
Values sent between devices are 32-bit elements; how exact they have to be, the bound alone decides.
No kernel may reach another device: no remote copies, remote signals or barrier semaphores. Data moves between devices by JAX's collectives and lax.ppermute only.
A program may use at most 128 MiB of HBM per device.

```python
import math
import jax
import jax.numpy as jnp
from jax import lax

ROWS = 128
COLS = 2048
DEPTH_DEV = 8
DEPTHS = 2048
N_GROUP = 16
N_MEMBER = 16


def plant(result, rng, low, high):
    longest = result.shape.index(max(result.shape))
    spots = []
    for shift in (0, 1):
        where = [jax.random.randint(jax.random.fold_in(rng, axis), (), 0, length) for axis, length in enumerate(result.shape)]
        where[longest] = (where[longest] + shift) % result.shape[longest]
        spots.append(tuple(where))
    return result.at[spots[0]].set(low).at[spots[1]].set(high)


def level_of(own_key, extent, split, smallest, largest):
    gain = 1.0
    for position, parts in split:
        heights = jax.random.uniform(jax.random.fold_in(jax.random.fold_in(own_key, 6), position), (parts,), jnp.float32, smallest / len(split), largest / len(split))
        gain = gain * jnp.repeat(jnp.exp(heights), extent[position] // parts).reshape((-1,) + (1,) * (len(extent) - 1 - position))
    return gain


def scatter_about(rng, shape, spread, limit, shards=(), kind=jnp.bfloat16):
    gain = level_of(rng, shape, shards, -0.22, 0.18) if shards else 1.0
    drawn = jax.random.normal(rng, shape, jnp.float32) * spread * gain
    return jnp.minimum(jnp.maximum(drawn, -limit), limit).astype(kind)


def setup_inputs(seed: int = 0) -> dict:
    keys = jax.random.split(jax.random.key(seed), 5)
    return {
        "level_set": scatter_about(keys[0], (DEPTHS, ROWS, COLS), 1.0, 6.0, ((0, 256),)),
        "ray_length": plant(jax.random.randint(keys[1], (ROWS, COLS), DEPTHS // 4, DEPTHS + 1), jax.random.fold_in(keys[1], 1), DEPTHS // 4, DEPTHS).astype(jnp.int32),
        "member_flip": plant(jax.random.randint(keys[2], (N_GROUP,), 0, N_MEMBER), jax.random.fold_in(keys[2], 1), 0, N_MEMBER - 1).astype(jnp.int32),
        "group_flip": jax.random.randint(keys[3], (1,), 0, N_GROUP * N_MEMBER).astype(jnp.int32),
    }


def march_slab(slab_values, first_sample, ray_length, depths, member_count):
    slices = slab_values.shape[0]
    level_values = slab_values.astype(jnp.float32)
    padded = jnp.pad(level_values, ((0, 0), (1, 1), (1, 1)), mode='edge')
    across = (padded[:, 1:-1, 2:] - padded[:, 1:-1, :-2]) * 0.5
    downward = (padded[:, 2:, 1:-1] - padded[:, :-2, 1:-1]) * 0.5
    facing = (0.48 * across + 0.6 * downward + 0.64) * lax.rsqrt(across * across + downward * downward + 1.0)
    shading = 0.25 + 0.75 * jnp.maximum(facing, 0.0)
    sample = first_sample.astype(jnp.int32) + jnp.arange(slices, dtype=jnp.int32)
    active_mask = sample[:, None, None] < ray_length[None, :, :]
    opacity = jnp.where(active_mask, 9.0 / depths * jnp.exp(-4.0 * level_values * level_values), jnp.float32(0.0))
    through = jnp.cumprod(1.0 - opacity, axis=0)
    before = jnp.concatenate([jnp.ones_like(through[:1]), through[:-1]], axis=0)
    weight = before * opacity
    sample_real = sample.astype(jnp.float32)
    phase_angle = 2.0 * math.pi / (slices * member_count) * sample_real
    channel_shift = 2.0 * math.pi / 3.0 * jnp.arange(3, dtype=jnp.float32)
    banding = 0.5 + 0.5 * jnp.cos(phase_angle[None, :] + channel_shift[:, None])
    colors = jnp.tensordot(banding, weight * shading, axes=1, precision=lax.Precision.HIGHEST)
    distance = jnp.tensordot((sample_real + 0.5) / depths, weight, axes=1, precision=lax.Precision.HIGHEST)
    return jnp.concatenate([colors, distance[None], (1.0 - through[-1])[None]], axis=0)

def reference(level_set, ray_length, member_flip, group_flip):
    whole_flip = group_flip[0].astype(jnp.int32)
    high_flip = whole_flip // N_MEMBER
    low_flip = whole_flip % N_MEMBER

    def visit_slab(step_index, carry):
        shaded, transmit = carry
        depth_rank = jnp.asarray(step_index).astype(jnp.int32)
        group_rank = depth_rank // N_MEMBER
        member_rank = depth_rank % N_MEMBER
        group_id = jnp.bitwise_xor(group_rank, high_flip)
        member_id = jnp.bitwise_xor(jnp.bitwise_xor(member_rank, low_flip), member_flip[group_id])
        start_row = ((group_id * N_MEMBER + member_id) * DEPTH_DEV).astype(jnp.int32)
        slab_values = lax.dynamic_slice_in_dim(level_set, start_row, DEPTH_DEV, 0)
        partial_value = march_slab(slab_values, depth_rank * DEPTH_DEV, ray_length, DEPTHS, N_MEMBER)
        shaded = shaded + transmit[None] * partial_value[:4]
        transmit = transmit * (1.0 - partial_value[4])
        return (shaded, transmit)
    start_state = (jnp.zeros((4, ROWS, COLS), jnp.float32), jnp.ones((ROWS, COLS), jnp.float32))
    shaded, transmit = lax.fori_loop(0, N_GROUP * N_MEMBER, visit_slab, start_state)
    final_image = jnp.concatenate([shaded, (1.0 - transmit)[None]], axis=0)
    return final_image.reshape(5, ROWS * COLS)
```

```python
import functools
import math

import jax
import jax.numpy as jnp
from jax import lax
from jax.experimental import pallas as pl
from jax.experimental.pallas import tpu as pltpu
from jax.sharding import PartitionSpec as P

LANES = 128
CH = 5


def march_kernel(with_merge, j0, nj, last_tile, sc, coef, lvl_hbm, ray_ref, *refs):
    if with_merge:
        other_ref, keep_ref, send_ref, raw, level, stage, sem = refs
    else:
        out_ref, raw, level, sem = refs
    depth = lvl_hbm.shape[0]
    tiles = 8
    step = pl.program_id(0)
    half = sc[0]
    first = sc[1]
    shift = sc[2]
    lo = 1 if j0 > 0 else 0
    hi = 1 if j0 + nj <= last_tile else 0
    total = lo + nj + hi

    def fetch(slot):
        row = pl.multiple_of((j0 - lo + slot) * 16, 16)
        col = pl.multiple_of(half * (7 * LANES), LANES)
        return pltpu.make_async_copy(
            lvl_hbm.at[:, pl.ds(row, 16), pl.ds(col, 9 * LANES)],
            raw.at[slot],
            sem.at[slot],
        )

    def convert(slot, part):
        base = pl.multiple_of((slot - lo) * 16 + 8, 8)

        @pl.loop(0, depth)
        def _(k):
            def put(tile, value):
                if part == 0:
                    level[k, tile, pl.ds(base, 16), :] = value
                elif part == 1:
                    level[k, tile, pl.ds(0, 8), :] = value[8:]
                else:
                    level[k, tile, pl.ds(base, 8), :] = value[:8]

            for q in range(9):
                value = raw[slot, k, :, q * LANES : (q + 1) * LANES].astype(jnp.float32)
                put(q + 1 - half, value)
                if q == 0:
                    left = value[:, :1]
                if q == 8:
                    right = value[:, LANES - 1 :]
            edge = jnp.where(half == 0, left, right)
            put(9 * half, jnp.broadcast_to(edge, (16, LANES)))

    @pl.when(step == 0)
    def _():
        for slot in range(total):
            fetch(slot).start()
        if lo:
            fetch(0).wait()
            convert(0, 1)
        fetch(lo).wait()
        convert(lo, 0)
        if not lo:

            @pl.loop(0, depth)
            def _(k):
                for q in range(10):
                    level[k, q, 7:8, :] = level[k, q, 8:9, :]

    @pl.when(step + 1 < nj)
    def _():
        fetch(step + 1 + lo).wait()
        convert(step + 1 + lo, 0)

    @pl.when(step + 1 == nj)
    def _():
        if hi:
            fetch(total - 1).wait()
            convert(total - 1, 2)
        else:
            end = nj * 16 + 8

            @pl.loop(0, depth)
            def _(k):
                for q in range(10):
                    level[k, q, end : end + 1, :] = level[k, q, end - 1 : end, :]

    lane = lax.broadcasted_iota(jnp.int32, (8, LANES), 1)
    is_first = lane == 0
    is_last = lane == LANES - 1
    if with_merge:
        target = stage
    else:
        target = out_ref.reshape(8 * 2 * CH * tiles, LANES)

    @pl.loop(0, 2)
    def _(u):
        row = step * 16 + u * 8 + 8
        for ct in range(tiles):
            ahead = ray_ref[pl.ds(pl.multiple_of(u * 8, 8), 8), ct * LANES : (ct + 1) * LANES] - first
            through = None
            red = green = blue = far = None
            for k in range(depth):
                mid = level[k, ct + 1, pl.ds(pl.multiple_of(row, 8), 8), :]
                up = level[k, ct + 1, pl.ds(row - 1, 8), :]
                down = level[k, ct + 1, pl.ds(row + 1, 8), :]
                before = level[k, ct, pl.ds(pl.multiple_of(row, 8), 8), :]
                after = level[k, ct + 2, pl.ds(pl.multiple_of(row, 8), 8), :]
                left = pltpu.roll(jnp.where(is_last, before, mid), 1, 1)
                right = pltpu.roll(jnp.where(is_first, after, mid), LANES - 1, 1)
                dc = right - left
                dr = down - up
                slope = dc * dc + dr * dr
                norm = lax.rsqrt(slope * 0.25 + 1.0)
                facing = (dc * 0.18 + dr * 0.225 + 0.48) * norm
                shade = jnp.maximum(facing, 0.0) + 0.25
                opacity = (9.0 / 2048.0) * jnp.exp(mid * mid * -4.0)
                opacity = jnp.where(ahead > k, opacity, 0.0)
                if k == 0:
                    weight = opacity
                    through = 1.0 - opacity
                else:
                    weight = through * opacity
                    through = through - weight
                lit = weight * shade
                terms = [lit * coef[k, 0], lit * coef[k, 1], lit * coef[k, 2], weight * coef[k, 3]]
                if k == 0:
                    red, green, blue, far = terms
                else:
                    red, green, blue, far = red + terms[0], green + terms[1], blue + terms[2], far + terms[3]
            for c, value in enumerate((red, green, blue, far, through)):
                start = u * (CH * tiles) + c * tiles + ct
                target[pl.ds(start, 8, stride=2 * CH * tiles), :] = pltpu.roll(value, shift, 0)

    if with_merge:
        mine_front = sc[3] == 1

        @pl.loop(0, 2)
        def _(u):
            for z in range(8):
                mine, theirs = [], []
                for c in range(CH):
                    start = pl.multiple_of(z * (2 * CH * tiles) + u * (CH * tiles) + c * tiles, 8)
                    mine.append(stage[pl.ds(start, 8), :])
                    theirs.append(other_ref[z, u, c])
                lead = jnp.where(mine_front, mine[4], theirs[4])
                into = keep_ref if z < 4 else send_ref
                for c in range(4):
                    front = jnp.where(mine_front, mine[c], theirs[c])
                    back = jnp.where(mine_front, theirs[c], mine[c])
                    into[z % 4, u, c] = front + lead * back
                into[z % 4, u, 4] = mine[4] * theirs[4]


def march(scalars, coef, level_set, ray_length, other, j0, nj):
    depth, rows, cols = level_set.shape
    last_tile = rows // 16 - 1
    slots = nj + (1 if j0 > 0 else 0) + (1 if j0 + nj <= last_tile else 0)
    width = cols // 2
    groups = 2 * nj
    in_specs = [
        pl.BlockSpec(memory_space=pltpu.SMEM),
        pl.BlockSpec(memory_space=pl.ANY),
        pl.BlockSpec((16, width), lambda i, s: (j0 + i, s[0])),
    ]
    scratch = [
        pltpu.VMEM((slots, depth, 16, 9 * LANES), jnp.bfloat16),
        pltpu.VMEM((depth, 10, nj * 16 + 16, LANES), jnp.float32),
    ]
    args = [coef, level_set, ray_length]
    if other is None:
        out_shape = jax.ShapeDtypeStruct((8, groups, CH, 8, LANES), jnp.float32)
        out_specs = pl.BlockSpec((8, 2, CH, 8, LANES), lambda i, s: (0, i, 0, 0, 0))
    else:
        args.append(other)
        in_specs.append(pl.BlockSpec((8, 2, CH, 8, LANES), lambda i, s: (0, i, 0, 0, 0)))
        out_shape = [jax.ShapeDtypeStruct((4, groups, CH, 8, LANES), jnp.float32)] * 2
        out_specs = [pl.BlockSpec((4, 2, CH, 8, LANES), lambda i, s: (0, i, 0, 0, 0))] * 2
        scratch.append(pltpu.VMEM((8 * 2 * CH * 8, LANES), jnp.float32))
    scratch.append(pltpu.SemaphoreType.DMA((slots,)))
    pixels = groups * 8 * width
    return pl.pallas_call(
        functools.partial(march_kernel, other is not None, j0, nj, last_tile),
        grid_spec=pltpu.PrefetchScalarGridSpec(
            num_scalar_prefetch=1, grid=(nj,), in_specs=in_specs, out_specs=out_specs, scratch_shapes=scratch
        ),
        out_shape=out_shape,
        compiler_params=pltpu.CompilerParams(dimension_semantics=("arbitrary",)),
        cost_estimate=pl.CostEstimate(flops=pixels * depth * 40, bytes_accessed=pixels * 40, transcendentals=pixels * 16),
        name="march_merge" if other is not None else "march_send",
    )(scalars, *args)


def pair_kernel(sc, keep_ref, got_ref, *outs):
    odd = sc[0] == 1
    mine_front = sc[1] == 1
    for j, out in enumerate(outs):
        i = jnp.where(odd, j, 3 - j)

        @pl.loop(0, keep_ref.shape[1])
        def _(g):
            mine = [keep_ref[i, g, c] for c in range(CH)]
            theirs = [got_ref[i, g, c] for c in range(CH)]
            lead = jnp.where(mine_front, mine[4], theirs[4])
            for c in range(4):
                front = jnp.where(mine_front, mine[c], theirs[c])
                back = jnp.where(mine_front, theirs[c], mine[c])
                out[g, c] = front + lead * back
            out[g, 4] = mine[4] * theirs[4]


def merge_pair(scalars, keep, got):
    groups = keep.shape[1]
    block = min(4, groups)
    spec = pl.BlockSpec((4, block, CH, 8, LANES), lambda i, s: (0, i, 0, 0, 0))
    return pl.pallas_call(
        pair_kernel,
        grid_spec=pltpu.PrefetchScalarGridSpec(
            num_scalar_prefetch=1,
            grid=(groups // block,),
            in_specs=[spec, spec],
            out_specs=[pl.BlockSpec((block, CH, 8, LANES), lambda i, s: (i, 0, 0, 0))] * 4,
        ),
        out_shape=[jax.ShapeDtypeStruct((groups, CH, 8, LANES), jnp.float32)] * 4,
        name="merge_pair",
    )(scalars, keep, got)


def quad_kernel(sc, a_ref, b_ref, c_ref, d_ref, out_ref):
    parts = (a_ref, b_ref, c_ref, d_ref)

    @pl.loop(0, a_ref.shape[0])
    def _(g):
        clear = [p[g, 4] for p in parts]
        total = [None] * 4
        for n, part in enumerate(parts):
            lead = None
            for o in range(4):
                if o != n:
                    factor = jnp.where(sc[o] < sc[n], clear[o], 1.0)
                    lead = factor if lead is None else lead * factor
            for c in range(4):
                term = lead * part[g, c]
                total[c] = term if n == 0 else total[c] + term
        for c in range(4):
            out_ref[g, c] = total[c]
        out_ref[g, 4] = (clear[0] * clear[1]) * (clear[2] * clear[3])


def merge_quad(scalars, parts):
    groups = parts[0].shape[0]
    block = min(8, groups)
    spec = pl.BlockSpec((block, CH, 8, LANES), lambda i, s: (i, 0, 0, 0))
    return pl.pallas_call(
        quad_kernel,
        grid_spec=pltpu.PrefetchScalarGridSpec(
            num_scalar_prefetch=1, grid=(groups // block,), in_specs=[spec] * 4, out_specs=spec
        ),
        out_shape=jax.ShapeDtypeStruct((groups, CH, 8, LANES), jnp.float32),
        name="merge_quad",
    )(scalars, *parts)


def final_kernel(sc, in_ref, out_ref):
    flip = sc[0]
    clear = None
    total = [None] * 4
    for r in range(in_ref.shape[0]):
        g = r ^ flip
        for c in range(4):
            value = in_ref[g, c]
            total[c] = value if r == 0 else total[c] + clear * value
        clear = in_ref[g, 4] if r == 0 else clear * in_ref[g, 4]
    total.append(1.0 - clear)
    for c in range(CH):
        for t in range(8):
            out_ref[c : c + 1, t * LANES : (t + 1) * LANES] = total[c][t : t + 1]


def finish(scalars, gathered):
    return pl.pallas_call(
        final_kernel,
        grid_spec=pltpu.PrefetchScalarGridSpec(
            num_scalar_prefetch=1,
            grid=(1,),
            in_specs=[pl.BlockSpec(gathered.shape, lambda i, s: (0, 0, 0, 0))],
            out_specs=pl.BlockSpec((CH, 8 * LANES), lambda i, s: (0, 0)),
        ),
        out_shape=jax.ShapeDtypeStruct((CH, 8 * LANES), jnp.float32),
        name="finish",
    )(scalars, gathered)


def member_route(move):
    route = []
    for m in range(16):
        z, core = m // 2, m % 2
        route.append((m, (move(z) % 8) * 2 + core))
    return route


def body(level_set, ray_length, member_flip, group_flip):
    depth = level_set.shape[0]
    members = lax.axis_size("member")
    depths = depth * members * lax.axis_size("group")
    group = lax.axis_index("group")
    member = lax.axis_index("member")
    z, core = member // 2, member % 2
    whole = group_flip[0]
    mask = member_flip[0] ^ (whole % members)
    group_mask = whole // members
    first = ((group ^ group_mask) * members + (member ^ mask)) * depth
    sample = first + jnp.arange(depth, dtype=jnp.int32)
    angle = (2.0 * math.pi / 128.0) * (sample % 128).astype(jnp.float32)
    offset = (2.0 * math.pi / 3.0) * jnp.arange(3, dtype=jnp.float32)
    bands = 0.5 + 0.5 * jnp.cos(angle[:, None] + offset[None, :])
    coef = jnp.concatenate([bands, ((sample.astype(jnp.float32) + 0.5) / depths)[:, None]], axis=1)
    odd = z % 2
    base = jnp.where(odd == 1, z, (z + 5) % 8)
    turn = (8 - base) % 8
    core_front = ((core ^ mask) & 1) == 0

    def packed(half):
        return jnp.stack([half, first, turn, core_front.astype(jnp.int32)]).astype(jnp.int32)

    rows = level_set.shape[1]
    nj = rows // 16
    send = march(packed(1 - core), coef, level_set, ray_length, None, 0, nj)
    other = lax.ppermute(send, "member", [(m, m ^ 1) for m in range(16)])
    keep, away = march(packed(core), coef, level_set, ray_length, other, 0, nj)
    got = lax.ppermute(away, "member", member_route(lambda s: s ^ 1))
    pair_front = ((z ^ (mask >> 1)) & 1) == 0
    pair = merge_pair(jnp.stack([odd, pair_front.astype(jnp.int32)]).astype(jnp.int32), keep, got)
    parts = [pair[0]]
    for j in (1, 2, 3):
        parts.append(lax.ppermute(pair[j], "member", member_route(lambda s: s + j if s % 2 else s - j)))
    p = z // 2
    even = jnp.stack([p, p - 1, p + 1, p + 2]) % 4
    uneven = jnp.stack([p, p + 1, p - 1, p + 2]) % 4
    ranks = jnp.where(odd == 1, uneven, even) ^ (mask >> 2)
    quad = merge_quad(ranks.astype(jnp.int32), parts)
    gathered = lax.all_to_all(quad, "group", 0, 0, tiled=True)
    return finish(group_mask.reshape(1).astype(jnp.int32), gathered)


def solution(mesh):
    in_specs = (P(("group", "member"), None, None), P(), P("group"), P())
    out_specs = P(None, ("group", "member"))
    return jax.shard_map(body, mesh=mesh, in_specs=in_specs, out_specs=out_specs, check_vma=False)
```

```python
import functools
import math

import jax
import jax.numpy as jnp
import numpy as np
from jax import lax
from jax.experimental import pallas as pl
from jax.experimental.pallas import tpu as pltpu
from jax.sharding import PartitionSpec as P


LANES = 128
CH = 5
CHUNKS = (3, 3, 2)


def place(member_flip, group_flip, members):
    group, member = lax.axis_index("group"), lax.axis_index("member")
    mask = member_flip ^ (group_flip & (members - 1))
    group_mask = lax.shift_right_logical(group_flip, members.bit_length() - 1)
    return group, member, mask, group_mask


def march_kernel(with_merge, resident, j0, nj, last_tile, members, depths, mf, gf, table, lvl, ray, *refs):
    if with_merge:
        other, refs = refs[0], refs[1:]
    if resident:
        refs = refs[1:]
    if with_merge:
        keep_ref, send_ref, mark_ref, level, stage = refs[:5]
        refs = refs[5:]
        mark_ref[...] = jnp.zeros_like(mark_ref)
    else:
        out_ref, level = refs[:2]
        refs = refs[2:]
    if not resident:
        raw, rays, sem, ray_sem = refs
    depth = lvl.shape[0]
    group, member, mask, group_mask = place(mf[0], gf[0], members)
    core = member & 1
    z = lax.shift_right_logical(member, 1)
    half = core if with_merge else 1 - core
    rank = member ^ mask
    first = ((group ^ group_mask) * members + rank) * depth
    base = jnp.where((z & 1) == 1, z, z + 5)
    shift = (8 - base) & 7
    lo = 1 if j0 > 0 else 0
    hi = 1 if j0 + nj <= last_tile else 0
    total = lo + nj + hi
    left_col = half * (7 * LANES)
    ray_col = half * (8 * LANES)

    def fetch(slot):
        row = pl.multiple_of((j0 - lo + slot) * 16, 16)
        return pltpu.make_async_copy(
            lvl.at[:, pl.ds(row, 16), pl.ds(pl.multiple_of(left_col, LANES), 9 * LANES)], raw.at[slot], sem.at[slot]
        )

    def arrive(slot):
        if not resident:
            fetch(slot).wait()

    def fetch_rays():
        return pltpu.make_async_copy(
            ray.at[pl.ds(j0 * 16, nj * 16), pl.ds(pl.multiple_of(ray_col, LANES), 8 * LANES)], rays, ray_sem.at[0]
        )

    def convert(slot, part):
        start = pl.multiple_of((slot - lo) * 16 + 8, 8)

        def put(k, tile, value):
            if part == 0:
                level[k, tile, pl.ds(start, 16), :] = value
            elif part == 1:
                level[k, tile, pl.ds(0, 8), :] = value[8:]
            else:
                level[k, tile, pl.ds(start, 8), :] = value[:8]

        for k in range(depth):
            for q in range(9):
                if resident:
                    row = pl.multiple_of((j0 - lo + slot) * 16, 16)
                    col = pl.multiple_of(left_col + q * LANES, LANES)
                    value = lvl[k, pl.ds(row, 16), pl.ds(col, LANES)].astype(jnp.float32)
                else:
                    value = raw[slot, k, :, q * LANES : (q + 1) * LANES].astype(jnp.float32)
                put(k, q + 1 - half, value)
                if q == 0:
                    left = value[:, :1]
                if q == 8:
                    right = value[:, LANES - 1 :]
            edge = jnp.where(half == 0, left, right)
            put(k, 9 * half, jnp.broadcast_to(edge, (16, LANES)))

    if not resident:
        for slot in [lo, *range(lo), *range(lo + 1, total)]:
            fetch(slot).start()
            if slot == lo:
                fetch_rays().start()
    arrive(lo)
    convert(lo, 0)
    if lo:
        arrive(0)
        convert(0, 1)
    else:
        for k in range(depth):
            for q in range(10):
                level[k, q, 7:8, :] = level[k, q, 8:9, :]
    if not resident:
        fetch_rays().wait()

    lane = lax.broadcasted_iota(jnp.int32, (8, LANES), 1)
    is_first = lane == 0
    is_last = lane == LANES - 1
    phase = (rank & (members - 1)) * (depth * 3)
    shade_of = [[table[phase + k * 3 + c] for c in range(3)] for k in range(depth)]
    start_real = first.astype(jnp.float32) + 0.5
    far_of = [(start_real + k) * (1.0 / depths) for k in range(depth)]
    mine_front = (rank & 1) == 0
    target = stage if with_merge else out_ref
    spread = (2 if with_merge else 2 * nj) * CH * 8

    def row_step(step, _):
        @pl.when(step + 1 < nj + hi)
        def _():
            arrive(step + 1 + lo)
            convert(step + 1 + lo, 0)

        if not hi:

            @pl.when(step + 1 == nj)
            def _():
                end = nj * 16 + 8
                for k in range(depth):
                    for q in range(10):
                        level[k, q, end : end + 1, :] = level[k, q, end - 1 : end, :]

        @pl.loop(0, 2)
        def _(u):
            row = step * 16 + u * 8 + 8
            place_row = (u if with_merge else 2 * step + u) * (CH * 8)
            for ct in range(8):
                if resident:
                    lengths = ray[pl.ds(pl.multiple_of(j0 * 16 + step * 16 + u * 8, 8), 8), pl.ds(pl.multiple_of(ray_col + ct * LANES, LANES), LANES)]
                else:
                    lengths = rays[pl.ds(pl.multiple_of(step * 16 + u * 8, 8), 8), ct * LANES : (ct + 1) * LANES]
                ahead = lengths - first
                for k in range(depth):
                    mid = level[k, ct + 1, pl.ds(pl.multiple_of(row, 8), 8), :]
                    up = level[k, ct + 1, pl.ds(row - 1, 8), :]
                    down = level[k, ct + 1, pl.ds(row + 1, 8), :]
                    before = level[k, ct, pl.ds(pl.multiple_of(row, 8), 8), :]
                    after = level[k, ct + 2, pl.ds(pl.multiple_of(row, 8), 8), :]
                    left = pltpu.roll(jnp.where(is_last, before, mid), 1, 1)
                    right = pltpu.roll(jnp.where(is_first, after, mid), LANES - 1, 1)
                    dc = right - left
                    dr = down - up
                    slope = dc * dc + dr * dr
                    norm = lax.rsqrt(slope * 0.25 + 1.0)
                    facing = (dc * 0.18 + dr * 0.225 + 0.48) * norm
                    shade = jnp.maximum(facing, 0.0) + 0.25
                    opacity = (9.0 / depths) * jnp.exp(mid * mid * -4.0)
                    opacity = jnp.where(ahead > k, opacity, 0.0)
                    if k == 0:
                        weight = opacity
                        through = 1.0 - opacity
                    else:
                        weight = through * opacity
                        through = through - weight
                    lit = weight * shade
                    terms = [lit * shade_of[k][0], lit * shade_of[k][1], lit * shade_of[k][2], weight * far_of[k]]
                    sums = terms if k == 0 else [a + b for a, b in zip(sums, terms)]
                for c, value in enumerate(sums + [through]):
                    target[pl.ds(place_row + c * 8 + ct, 8, stride=spread), :] = pltpu.roll(value, shift, 0)

        if with_merge:

            @pl.loop(0, 2)
            def _(u):
                g = 2 * step + u
                for d in range(8):
                    mine, theirs = [], []
                    for c in range(CH):
                        at = pl.multiple_of(d * spread + u * (CH * 8) + c * 8, 8)
                        mine.append(stage[pl.ds(at, 8), :])
                        theirs.append(other[d, g, c])
                    lead = jnp.where(mine_front, mine[4], theirs[4])
                    into = keep_ref if d < 4 else send_ref
                    for c in range(4):
                        front = jnp.where(mine_front, mine[c], theirs[c])
                        back = jnp.where(mine_front, theirs[c], mine[c])
                        into[d % 4, g, c] = front + lead * back
                    into[d % 4, g, 4] = mine[4] * theirs[4]

        return 0

    lax.fori_loop(0, nj, row_step, 0)


def march(member_flip, group_flip, table, level_set, ray_length, other, mark, j0, nj, members, depths):
    depth, rows, cols = level_set.shape
    last_tile = rows // 16 - 1
    slots = nj + (1 if j0 > 0 else 0) + (1 if j0 + nj <= last_tile else 0)
    groups = 2 * nj
    merge = other is not None
    resident = mark is not None
    smem = pl.BlockSpec(memory_space=pltpu.SMEM)
    vmem = pl.BlockSpec(memory_space=pltpu.VMEM)
    hbm = pl.BlockSpec(memory_space=pltpu.MemorySpace.HBM)
    big = vmem if resident else hbm
    args = [member_flip, group_flip, table, level_set, ray_length]
    scratch = [pltpu.VMEM((depth, 10, nj * 16 + 24, LANES), jnp.float32)]
    mark_shape = jax.ShapeDtypeStruct((8, LANES), jnp.float32)
    if merge:
        args.append(other.reshape(8, groups, CH, 8, LANES))
        out_shape = [jax.ShapeDtypeStruct((4, groups, CH, 8, LANES), jnp.float32)] * 2 + [mark_shape]
        out_specs = [vmem] * 3
        scratch.append(pltpu.VMEM((8 * 2 * CH * 8, LANES), jnp.float32))
    else:
        out_shape = jax.ShapeDtypeStruct((8 * groups * CH * 8, LANES), jnp.float32)
        out_specs = vmem
    if resident:
        args.append(mark)
    else:
        scratch += [
            pltpu.VMEM((slots, depth, 16, 9 * LANES), jnp.bfloat16),
            pltpu.VMEM((nj * 16, 8 * LANES), jnp.int32),
            pltpu.SemaphoreType.DMA((slots,)),
            pltpu.SemaphoreType.DMA((1,)),
        ]
    pixels = groups * 8 * cols // 2
    return pl.pallas_call(
        functools.partial(march_kernel, merge, resident, j0, nj, last_tile, members, depths),
        in_specs=[smem] * 3 + [big] * 2 + [vmem] * (len(args) - 5),
        out_specs=out_specs,
        out_shape=out_shape,
        scratch_shapes=scratch,
        compiler_params=pltpu.CompilerParams(vmem_limit_bytes=(24 << 20) if resident else 65_800_000),
        cost_estimate=pl.CostEstimate(flops=pixels * depth * 40, bytes_accessed=pixels * 40, transcendentals=pixels * 16),
        name="march_merge" if merge else "march_send",
    )(*args)


def touch_kernel(lvl, ray, mark_ref):
    mark_ref[...] = jnp.zeros_like(mark_ref)


def touch(level_set, ray_length):
    vmem = pl.BlockSpec(memory_space=pltpu.VMEM)
    return pl.pallas_call(
        touch_kernel,
        in_specs=[vmem] * 2,
        out_specs=vmem,
        out_shape=jax.ShapeDtypeStruct((8, LANES), jnp.float32),
        compiler_params=pltpu.CompilerParams(vmem_limit_bytes=1 << 20),
        name="touch",
    )(level_set, ray_length)


def pair_kernel(members, mf, gf, keep, got, _, *refs):
    outs, mark_ref = refs[:4], refs[4]
    mark_ref[...] = jnp.zeros_like(mark_ref)
    _, member, mask, _ = place(mf[0], gf[0], members)
    z = lax.shift_right_logical(member, 1)
    odd = (z & 1) == 1
    mine_front = (lax.shift_right_logical(member ^ mask, 1) & 1) == 0

    @pl.loop(0, keep.shape[1] // 2)
    def _(n):
        for j, out in enumerate(outs):
            i = jnp.where(odd, j, 3 - j)
            for u in range(2):
                g = 2 * n + u
                mine = [keep[i, g, c] for c in range(CH)]
                theirs = [got[i, g, c] for c in range(CH)]
                lead = jnp.where(mine_front, mine[4], theirs[4])
                for c in range(4):
                    front = jnp.where(mine_front, mine[c], theirs[c])
                    back = jnp.where(mine_front, theirs[c], mine[c])
                    out[g, c] = front + lead * back
                out[g, 4] = mine[4] * theirs[4]


def merge_pair(member_flip, group_flip, keep, got, mark, members):
    groups = keep.shape[1]
    vmem = pl.BlockSpec(memory_space=pltpu.VMEM)
    smem = pl.BlockSpec(memory_space=pltpu.SMEM)
    return pl.pallas_call(
        functools.partial(pair_kernel, members),
        in_specs=[smem, smem, vmem, vmem, vmem],
        out_specs=[vmem] * 5,
        out_shape=[jax.ShapeDtypeStruct((groups, CH, 8, LANES), jnp.float32)] * 4 + [jax.ShapeDtypeStruct((8, LANES), jnp.float32)],
        cost_estimate=pl.CostEstimate(flops=keep.size * 8, bytes_accessed=keep.size * 12, transcendentals=0),
        compiler_params=pltpu.CompilerParams(vmem_limit_bytes=12 << 20),
        name="merge_pair",
    )(member_flip, group_flip, keep, got, mark)


def quad_kernel(counts, members, mf, gf, *refs):
    out = refs[-1]
    _, member, mask, _ = place(mf[0], gf[0], members)
    z = lax.shift_right_logical(member, 1)
    p = lax.shift_right_logical(z, 1)
    step = jnp.where((z & 1) == 1, 1, -1)
    flip = lax.shift_right_logical(mask, 2)
    ranks = [(q & 3) ^ flip for q in (p, p + step, p - step, p + 2)]
    begin = 0
    for n, count in enumerate(counts):
        local = refs[4 * n : 4 * n + 4]

        @pl.loop(0, count // 2)
        def _(h, local=local, begin=begin):
            for u in range(2):
                g = 2 * h + u
                clear = [part[g, 4] for part in local]
                total = [None] * 4
                for a in range(4):
                    lead = None
                    for o in range(4):
                        if o != a:
                            factor = jnp.where(ranks[o] < ranks[a], clear[o], 1.0)
                            lead = factor if lead is None else lead * factor
                    for c in range(4):
                        term = lead * local[a][g, c]
                        total[c] = term if a == 0 else total[c] + term
                for c in range(4):
                    out[begin + g, c] = total[c]
                out[begin + g, 4] = (clear[0] * clear[1]) * (clear[2] * clear[3])

        begin += count


def merge_quad(member_flip, group_flip, chunks, members):
    counts = [chunk[0].shape[0] for chunk in chunks]
    flat = [part for chunk in chunks for part in chunk]
    vmem = pl.BlockSpec(memory_space=pltpu.VMEM)
    smem = pl.BlockSpec(memory_space=pltpu.SMEM)
    return pl.pallas_call(
        functools.partial(quad_kernel, counts, members),
        in_specs=[smem, smem] + [vmem] * len(flat),
        out_specs=vmem,
        out_shape=jax.ShapeDtypeStruct((sum(counts), CH, 8, LANES), jnp.float32),
        compiler_params=pltpu.CompilerParams(vmem_limit_bytes=12 << 20),
        name="merge_quad",
    )(member_flip, group_flip, *flat)


def final_kernel(members, mf, gf, local, out_ref):
    _, _, _, flip = place(mf[0], gf[0], members)
    clear = None
    total = [None] * 4
    for r in range(local.shape[0]):
        g = r ^ flip
        for c in range(4):
            value = local[g, c]
            total[c] = value if r == 0 else total[c] + clear * value
        clear = local[g, 4] if r == 0 else clear * local[g, 4]
    total.append(1.0 - clear)
    for c in range(CH):
        for t in range(8):
            out_ref[c : c + 1, t * LANES : (t + 1) * LANES] = total[c][t : t + 1]


def finish(member_flip, group_flip, gathered, members):
    smem = pl.BlockSpec(memory_space=pltpu.SMEM)
    return pl.pallas_call(
        functools.partial(final_kernel, members),
        in_specs=[smem, smem, pl.BlockSpec(memory_space=pltpu.VMEM)],
        out_specs=pl.BlockSpec(memory_space=pltpu.VMEM),
        out_shape=jax.ShapeDtypeStruct((CH, 8 * LANES), jnp.float32),
        compiler_params=pltpu.CompilerParams(vmem_limit_bytes=8 << 20),
        name="finish",
    )(member_flip, group_flip, gathered)


def member_route(move):
    route = []
    for m in range(16):
        z, core = m // 2, m % 2
        route.append((m, (move(z) % 8) * 2 + core))
    return route


def body(level_set, ray_length, member_flip, group_flip):
    depth = level_set.shape[0]
    members, groups = lax.axis_size("member"), lax.axis_size("group")
    depths = depth * members * groups
    angle = (2.0 * math.pi / (depth * members)) * np.arange(depth * members)
    bands = 0.5 + 0.5 * np.cos(angle[:, None] + (2.0 * math.pi / 3.0) * np.arange(3)[None, :])
    table = jnp.asarray(bands.reshape(-1), jnp.float32)
    flips = (member_flip, group_flip)
    count = len(CHUNKS)
    begin = [sum(CHUNKS[:n]) for n in range(count)]
    keeps, aways, parts = {}, {}, []
    marks = {}
    last = None

    def slab(n):
        nonlocal last
        where = (begin[n], CHUNKS[n], members, depths)
        send = march(*flips, table, level_set, ray_length, None, marks.get(last), *where)
        other = lax.ppermute(send, "member", [(m, m ^ 1) for m in range(members)])
        if n == 0:
            marks["touch"] = touch(level_set, ray_length)
        keeps[n], aways[n], marks[f"march{n}"] = march(*flips, table, level_set, ray_length, other, marks["touch"] if n == 0 else marks[last], *where)
        last = f"march{n}"

    got = None
    slab(0)
    for n in range(count):
        away = aways[n]
        got = lax.ppermute(away, "member", member_route(lambda s: s ^ 1))
        if n == 0 and count > 1:
            slab(1)
        *pair, marks[f"pair{n}"] = merge_pair(*flips, keeps[n], got, marks[last], members)
        last = f"pair{n}"
        chunk = [pair[0]]
        for j in (3, 2, 1):
            chunk.insert(1, lax.ppermute(pair[j], "member", member_route(lambda s: s + j if s % 2 else s - j)))
        parts.append(chunk)
        if n + 2 < count:
            slab(n + 2)
    quad = merge_quad(*flips, parts, members)
    gathered = lax.all_to_all(quad, "group", 0, 0, tiled=True)
    return finish(*flips, gathered, members)


def solution(mesh):
    in_specs = (P(("group", "member"), None, None), P(), P("group"), P())
    out_specs = P(None, ("group", "member"))

    return jax.shard_map(body, mesh=mesh, in_specs=in_specs, out_specs=out_specs, check_vma=False)
```
